32 devices in a mesh: group: 2 (over y), quad: 2 (over core), rows: 8 (over z, x).
Axes of the slice: x: 2, y: 2, z: 4, core: 2. Of those that a mesh axis runs over, the one named last changes fastest.
Arguments:
- solutions: bfloat16 [32, 20480, 128], P('quad', ('group', 'rows')), parts along dimension 1, may hold values from -24 to 24
- point_of_slot: int32 [64], P(('group', 'quad')), parts along dimension 0, may hold values from 0 to 31, each once
- mass_blocks: bfloat16 [160, 20, 128, 128], P(('group', 'rows')), parts along dimension 0, may hold values from -0.125 to 0.125
- block_cols: int32 [160, 20], P(('group', 'rows')), parts along dimension 0, may hold values from 0 to 79, as said below
- sources: bfloat16 [20480, 64], P(('group', 'rows')), parts along dimension 0, may hold values from -0.0625 to 0.0625
Outputs:
- mass_applied: bfloat16 [8, 20480, 128], P('quad', ('group', 'rows')), parts along dimension 1
- reduced: float32 [16, 64, 128], P(('group', 'quad')), parts along dimension 0
The draws below stay inside these ranges and needn't reach their ends.
There are 2 independent parts, one for each index of `group`. The reference program is written for one: setup_inputs(seed, part) draws one part's arguments, and reference() takes and returns one part's arrays. A program takes and returns all parts, laid end to end along the dimension named above; each array names one. Nothing has to cross between parts.
Inputs may be any that keep to these rules, and one draw needn't show every extreme that they name: `point_of_slot`: each contour point sits in exactly one slot. `block_cols`: slot 0 of block row i holds i; every entry c of block row i has |c - i| <= 10; entries of a block row may repeat.
All inputs are finite; a program needn't handle non-finite values.
Results may differ from the reference program's by a relative error of at most 0.0063.
Values may be sent and summed in bfloat16 or wider, within the bound.
A program may use at most 128 MiB of HBM per device.

```python
import math
import jax
import jax.numpy as jnp
from jax import lax

ROWS_DEV = 1280
POINTS_DEV = 16
MOMENTS = 8
COLUMNS = 64
BLOCK = 128
SLOTS = 20
POINTS = 32
NBLOCKS = 80
ORDER = 10240
N_QUAD = 2


def draw_block_cols(key, part):
    span_blocks = ROWS_DEV // BLOCK
    row_index = jnp.arange(NBLOCKS, dtype=jnp.int32)[:, None]
    lowest = jnp.maximum(row_index - span_blocks, 0)
    highest = jnp.minimum(row_index + span_blocks, NBLOCKS - 1)
    random_bits = jax.random.randint(jax.random.fold_in(key, 7), (NBLOCKS, SLOTS - 1), 0, 1 << 20, dtype=jnp.int32)
    picked = lowest + random_bits % (highest - lowest + 1)
    return jnp.concatenate([row_index, picked], axis=1).astype(jnp.int32)


def levels(own_key, shape, cuts, smallest, high):
    def one(position, blocks):
        heights = jax.random.uniform(jax.random.fold_in(jax.random.fold_in(own_key, 6), position), (blocks,), jnp.float32, smallest / len(cuts), high / len(cuts))
        return jnp.repeat(jnp.exp(heights), shape[position] // blocks).reshape((-1,) + (1,) * (len(shape) - position - 1))

    factor_of = one(*cuts[0])
    for cut in cuts[1:]:
        factor_of = factor_of * one(*cut)
    return factor_of


def gaussian(stream_key, extent, spread, reach, pieces=(), kind=jnp.bfloat16):
    array = spread * jax.random.normal(stream_key, extent, jnp.float32)
    if pieces:
        array = array * levels(stream_key, extent, pieces, -0.22, 0.18)
    return jnp.clip(array, -reach, reach).astype(kind)


def setup_inputs(seed: int = 0, part: int = 0) -> dict:
    splits = jax.random.split(jax.random.key(seed), 6)
    part_splits = jax.random.split(jax.random.fold_in(splits[5], part), 6)
    return {
        "solutions": gaussian(part_splits[0], (POINTS, ORDER, 2 * COLUMNS), 4.0, 24.0, ((0, 2), (1, 8))),
        "point_of_slot": jax.random.permutation(part_splits[1], POINTS).astype(jnp.int32),
        "mass_blocks": gaussian(part_splits[2], (NBLOCKS, SLOTS, BLOCK, BLOCK), (SLOTS * BLOCK) ** -0.5, 0.125, ((0, 8),)),
        "block_cols": draw_block_cols(jax.random.fold_in(jax.random.fold_in(splits[5], part), 71), part),
        "sources": gaussian(part_splits[4], (ORDER, COLUMNS), ORDER ** -0.5, 0.0625, ((0, 8),)),
    }


def reference(solutions, point_of_slot, mass_blocks, block_cols, sources):
    theta = 2.0 * math.pi * (point_of_slot.astype(jnp.float32) + 0.5) / POINTS
    powers = jnp.arange(1, MOMENTS + 1, dtype=jnp.float32)
    angles = powers[:, None] * theta[None, :]
    cosine = (jnp.cos(angles) / POINTS).astype(jnp.bfloat16)
    sine = (jnp.sin(angles) / POINTS).astype(jnp.bfloat16)
    real_part = solutions[:, :, :COLUMNS]
    imag_part = solutions[:, :, COLUMNS:]
    total = jnp.zeros((MOMENTS, ORDER, 2 * COLUMNS), jnp.float32)
    for group_index in range(N_QUAD):
        first = group_index * POINTS_DEV
        real_rows = real_part[first:first + POINTS_DEV].reshape(POINTS_DEV, ORDER * COLUMNS)
        imag_rows = imag_part[first:first + POINTS_DEV].reshape(POINTS_DEV, ORDER * COLUMNS)
        cos_group = cosine[:, first:first + POINTS_DEV]
        sin_group = sine[:, first:first + POINTS_DEV]
        out_real = jnp.dot(cos_group, real_rows, preferred_element_type=jnp.float32) - jnp.dot(sin_group, imag_rows, preferred_element_type=jnp.float32)
        out_imag = jnp.dot(sin_group, real_rows, preferred_element_type=jnp.float32) + jnp.dot(cos_group, imag_rows, preferred_element_type=jnp.float32)
        partial_value = jnp.concatenate([out_real.reshape(MOMENTS, ORDER, COLUMNS), out_imag.reshape(MOMENTS, ORDER, COLUMNS)], axis=2)
        total = total + partial_value.astype(jnp.bfloat16).astype(jnp.float32)
    moments = total.astype(jnp.bfloat16)
    moment_blocks = moments.reshape(MOMENTS, NBLOCKS, BLOCK, 2 * COLUMNS)

    def add_slot(accum, slot_index):
        columns_now = block_cols[:, slot_index]
        tiles = lax.dynamic_index_in_dim(mass_blocks, slot_index, 1, keepdims=False)
        chosen = moment_blocks[:, columns_now]
        accum = accum + jnp.einsum("bij,mbjc->mbic", tiles.astype(jnp.float32), chosen.astype(jnp.float32))
        return accum, None

    start = jnp.zeros((MOMENTS, NBLOCKS, BLOCK, 2 * COLUMNS), jnp.float32)
    accum, _ = lax.scan(add_slot, start, jnp.arange(SLOTS, dtype=jnp.int32))
    mass_applied = accum.astype(jnp.bfloat16).reshape(MOMENTS, ORDER, 2 * COLUMNS)
    reduced = jnp.einsum("nl,mnc->mlc", sources.astype(jnp.float32), mass_applied.astype(jnp.float32))
    return mass_applied, reduced
```

```python
import functools
import math

import jax
import jax.numpy as jnp
from jax import lax
from jax.experimental import pallas as pl
from jax.experimental.pallas import tpu as pltpu
from jax.sharding import PartitionSpec as P

MOMENTS = 8
TILE = 16
MESH = pl.DeviceIdType.MESH


def kernel(
    n, quads, span, owned, points, chunk_blocks, reduce_here,
    weight_ref, cols_ref, sources_ref, sol_hbm, mass_hbm,
    out_hbm, red_out,
    sol, mass, sources_t, own, theirs, received, out_buf, term, rs_buf, red, *rest,
):
    panels = rest[:owned]
    (sol_sem, mass_sem, out_sem, q_send, q_recv, h_send, h_recv,
     rs_send, rs_recv, ag_send, ag_recv) = rest[owned:]
    me = lax.axis_index("rows")
    quad = lax.axis_index("quad")
    rows_here, lanes = sol.shape[1:]
    half = lanes // 2
    block = rows_here // span
    chunks = span // chunk_blocks
    chunk_rows = chunk_blocks * block
    right = jnp.minimum(me + 1, n - 1)
    left = jnp.maximum(me - 1, 0)

    def sol_copy(c):
        rows = pl.ds(c * chunk_rows, chunk_rows)
        return pltpu.make_async_copy(sol_hbm.at[:, rows], sol.at[:, rows], sol_sem.at[c])

    mass_copy = pltpu.make_async_copy(mass_hbm, mass, mass_sem)
    for c in range(chunks):
        sol_copy(c).start()
    mass_copy.start()

    barrier = pltpu.get_barrier_semaphore()
    pl.semaphore_signal(barrier, inc=1, device_id={"quad": 1 - quad}, device_id_type=MESH)
    if reduce_here:
        for o in range(1, n):
            pl.semaphore_signal(
                barrier, inc=1, device_id={"rows": lax.rem(me + o, n)}, device_id_type=MESH
            )
        pl.semaphore_wait(barrier, n)
    else:
        for o in (1, n - 1):
            pl.semaphore_signal(
                barrier, inc=1, device_id={"rows": lax.rem(me + o, n)}, device_id_type=MESH
            )
        pl.semaphore_wait(barrier, 3)

    def quad_copy(c):
        rows = pl.ds(c * chunk_rows, chunk_rows)
        return pltpu.make_async_remote_copy(
            src_ref=theirs.at[:, rows], dst_ref=received.at[:, rows],
            send_sem=q_send.at[c], recv_sem=q_recv.at[c],
            device_id={"quad": 1 - quad}, device_id_type=MESH,
        )

    pieces = [[(c * chunk_blocks, chunk_blocks) for c in range(chunks)]]
    pieces += [[(0, span)] for _ in range(owned - 1)]
    index_of = {}
    for k in range(owned):
        for p in range(len(pieces[k])):
            index_of[k, p] = len(index_of)

    def halo(k, p, to_right):
        first, count = pieces[k][p]
        source = panels[k].at[pl.ds(span + first, count)]
        target = panels[k].at[pl.ds(first if to_right else 2 * span + first, count)]
        side = 0 if to_right else 1
        at = index_of[k, p]
        return pltpu.make_async_remote_copy(
            src_ref=source, dst_ref=target,
            send_sem=h_send.at[at, side], recv_sem=h_recv.at[at, side],
            device_id={"rows": right if to_right else left}, device_id_type=MESH,
        )

    def halo_start(k, p):
        @pl.when(me < n - 1)
        def _():
            halo(k, p, True).start()

        @pl.when(me > 0)
        def _():
            halo(k, p, False).start()

    def halo_sent(k):
        @pl.when(me < n - 1)
        def _():
            for p in range(len(pieces[k])):
                halo(k, p, True).wait_send()

        @pl.when(me > 0)
        def _():
            for p in range(len(pieces[k])):
                halo(k, p, False).wait_send()

    def halo_arrived(k):
        @pl.when(me > 0)
        def _():
            for p in range(len(pieces[k])):
                halo(k, p, True).wait_recv()

        @pl.when(me < n - 1)
        def _():
            for p in range(len(pieces[k])):
                halo(k, p, False).wait_recv()

    def weigh(c):
        def body(g, carry):
            first = pl.multiple_of(c * chunk_rows + g * 2 * TILE, 2 * TILE)
            second = pl.multiple_of(first + TILE, TILE)
            stacked = jnp.concatenate(
                [
                    sol[:, pl.ds(first, TILE), :].reshape(points * TILE, lanes),
                    sol[:, pl.ds(second, TILE), :].reshape(points * TILE, lanes),
                ],
                axis=1,
            )
            z = jnp.dot(weight_ref[...], stacked, preferred_element_type=jnp.float32)
            height = 2 * owned * TILE
            negative = lax.broadcasted_iota(jnp.int32, (height, lanes), 1) < half
            for h, start in ((0, first), (1, second)):
                straight = z[:height, h * lanes:(h + 1) * lanes]
                crossed = pltpu.roll(z[height:, h * lanes:(h + 1) * lanes], half, 1)
                value = straight + jnp.where(negative, -crossed, crossed)
                value = value.astype(jnp.bfloat16).reshape(2 * owned, TILE, lanes)
                own[:, pl.ds(start, TILE), :] = value[:owned]
                theirs[:, pl.ds(start, TILE), :] = value[owned:]
            return carry

        lax.fori_loop(0, chunk_rows // (2 * TILE), body, 0)

    def add_up(k, first, count):
        def body(b, carry):
            rows = pl.ds(pl.multiple_of(b * block, block), block)
            total = own[k, rows, :].astype(jnp.float32) + received[k, rows, :].astype(jnp.float32)
            panels[k][span + b] = total.astype(jnp.bfloat16)
            return carry

        lax.fori_loop(first, first + count, body, 0)

    def first_moment(c):
        quad_copy(c).wait_recv()
        add_up(0, c * chunk_blocks, chunk_blocks)
        halo_start(0, c)

    for c in range(chunks):
        sol_copy(c).wait()
        weigh(c)
        quad_copy(c).start()
        if c > 0:
            first_moment(c - 1)
    first_moment(chunks - 1)
    for k in range(1, owned):
        add_up(k, 0, span)
        if k == 1:
            halo_start(1, 0)
    sources_t[...] = sources_ref[...].astype(jnp.float32).T.astype(jnp.bfloat16)
    mass_copy.wait()
    slots = mass.shape[1]

    def apply_mass(k):
        panel = panels[k]

        def body(i, carry):
            left_side = jnp.concatenate([mass[i, j] for j in range(slots)], axis=1)
            right_side = jnp.concatenate([panel[cols_ref[i, j]] for j in range(slots)], axis=0)
            value = jnp.dot(left_side, right_side, preferred_element_type=jnp.float32)
            out_buf[k, pl.ds(pl.multiple_of(i * block, block), block), :] = value.astype(jnp.bfloat16)
            return carry

        lax.fori_loop(0, span, body, 0)

    def out_copy(k):
        return pltpu.make_async_copy(out_buf.at[k], out_hbm.at[k], out_sem.at[k])

    def rs_copy(k, o):
        return pltpu.make_async_remote_copy(
            src_ref=term.at[k, lax.rem(me + o, n)], dst_ref=rs_buf.at[k, o],
            send_sem=rs_send.at[k, o], recv_sem=rs_recv.at[k, o],
            device_id={"rows": lax.rem(me + o, n)}, device_id_type=MESH,
        )

    def ag_copy(k, o, origin):
        return pltpu.make_async_remote_copy(
            src_ref=red.at[k, origin], dst_ref=red.at[k, origin],
            send_sem=ag_send.at[k, o], recv_sem=ag_recv.at[k, o],
            device_id={"rows": lax.rem(me + o, n)}, device_id_type=MESH,
        )

    def project(k):
        value = jnp.dot(sources_t[...], out_buf[k], preferred_element_type=jnp.float32)
        if reduce_here:
            term[k] = value.reshape(term.shape[1:])
            for o in range(1, n):
                rs_copy(k, o).start()
        else:
            red_out[k] = value

    def reduce(k):
        total = term[k, me]
        for o in range(1, n):
            rs_copy(k, o).wait_recv()
            total = total + rs_buf[k, o]
        red[k, me] = total
        for o in range(1, n):
            ag_copy(k, o, me).start()

    for k in range(owned):
        if k + 1 < owned:
            if k > 0:
                halo_sent(k - 1)
                halo_start(k + 1, 0)
        halo_arrived(k)
        apply_mass(k)
        out_copy(k).start()
        project(k)
        if reduce_here and k > 0:
            reduce(k - 1)
    if reduce_here:
        reduce(owned - 1)
    for k in range(max(owned - 2, 0), owned):
        halo_sent(k)
    for c in range(chunks):
        quad_copy(c).wait_send()
    for k in range(owned):
        out_copy(k).wait()
        if reduce_here:
            for o in range(1, n):
                rs_copy(k, o).wait_send()
                ag_copy(k, o, me).wait_send()
                ag_copy(k, o, lax.rem(me + n - o, n)).wait_recv()
            red_out[k] = red[k].reshape(red_out.shape[1:])


def local(n, quads, solutions, point_of_slot, mass_blocks, block_cols, sources):
    points, rows_here, lanes = solutions.shape
    width = lanes // 2
    span, slots, block_size = mass_blocks.shape[:3]
    owned = MOMENTS // quads
    total_points = points * quads
    chunk_blocks = 2
    chunks = span // chunk_blocks
    reduce_here = n <= 8 and width % n == 0
    parts = n if reduce_here else 1
    theta = 2.0 * math.pi * (point_of_slot.astype(jnp.float32) + 0.5) / total_points
    order = (jnp.arange(MOMENTS) + owned * lax.axis_index("quad")) % MOMENTS
    angles = (order + 1).astype(jnp.float32)[:, None] * theta[None, :]
    cosine = (jnp.cos(angles) / total_points).astype(jnp.bfloat16)
    sine = (jnp.sin(angles) / total_points).astype(jnp.bfloat16)
    both = jnp.concatenate([cosine, sine], axis=0)
    weight = both[:, None, :, None] * jnp.eye(TILE, dtype=jnp.bfloat16)[None, :, None, :]
    weight = weight.reshape(2 * MOMENTS * TILE, points * TILE)
    cols = block_cols - (lax.axis_index("rows") - 1) * span

    bf16, f32 = jnp.bfloat16, jnp.float32
    dma = pltpu.SemaphoreType.DMA
    pieces = chunks + owned - 1
    vmem = pl.BlockSpec(memory_space=pltpu.VMEM)
    hbm = pl.BlockSpec(memory_space=pl.ANY)
    mass_applied, reduced = pl.pallas_call(
        functools.partial(kernel, n, quads, span, owned, points, chunk_blocks, reduce_here),
        out_shape=(
            jax.ShapeDtypeStruct((owned, rows_here, lanes), bf16),
            jax.ShapeDtypeStruct((owned, width, lanes), f32),
        ),
        in_specs=[vmem, pl.BlockSpec(memory_space=pltpu.SMEM), vmem, hbm, hbm],
        out_specs=(hbm, vmem),
        scratch_shapes=[
            pltpu.VMEM(solutions.shape, bf16),
            pltpu.VMEM(mass_blocks.shape, bf16),
            pltpu.VMEM((width, rows_here), bf16),
            pltpu.VMEM((owned, rows_here, lanes), bf16),
            pltpu.VMEM((owned, rows_here, lanes), bf16),
            pltpu.VMEM((owned, rows_here, lanes), bf16),
            pltpu.VMEM((owned, rows_here, lanes), bf16),
            pltpu.VMEM((owned, parts, width // parts, lanes), f32),
            pltpu.VMEM((owned, parts, width // parts, lanes), f32),
            pltpu.VMEM((owned, parts, width // parts, lanes), f32),
        ]
        + [pltpu.VMEM((3 * span, block_size, lanes), bf16) for _ in range(owned)]
        + [
            dma((chunks,)), dma, dma((owned,)), dma((chunks,)), dma((chunks,)),
            dma((pieces, 2)), dma((pieces, 2)),
            dma((owned, parts)), dma((owned, parts)), dma((owned, parts)), dma((owned, parts)),
        ],
        compiler_params=pltpu.CompilerParams(
            collective_id=0, has_side_effects=True, vmem_limit_bytes=48 * 1024 * 1024
        ),
    )(weight, cols, sources, solutions, mass_blocks)
    if not reduce_here:
        reduced = lax.psum(reduced, "rows")
    return mass_applied, reduced


def solution(mesh):
    in_specs = (
        P("quad", ("group", "rows"), None),
        P(("group", "quad")),
        P(("group", "rows"), None, None, None),
        P(("group", "rows"), None),
        P(("group", "rows"), None),
    )
    out_specs = (P("quad", ("group", "rows"), None), P(("group", "quad"), None, None))
    step = functools.partial(local, mesh.shape["rows"], mesh.shape["quad"])
    return jax.shard_map(step, mesh=mesh, in_specs=in_specs, out_specs=out_specs, check_vma=False)
```

```python
import functools
import math

import jax
import jax.numpy as jnp
from jax import lax
from jax.experimental import pallas as pl
from jax.experimental.pallas import tpu as pltpu
from jax.sharding import PartitionSpec as P

MOMENTS = 8
TILE = 16
WINDOW = 5
MESH = pl.DeviceIdType.MESH


def kernel(
    n, quads, span, owned, points, chunk_blocks, reduce_here,
    trig_ref, cols_ref, sources_ref, sol_hbm, mass_hbm,
    out_hbm, red_out,
    sol, mass, weight, own, theirs, received, out_buf, term, rs_buf, red, *rest,
):
    panels = rest[:owned]
    (sol_sem, mass_sem, out_sem, q_send, q_recv, x_send, x_recv, f_send, f_recv,
     rs_send, rs_recv, ag_send, ag_recv) = rest[owned:]
    me = lax.axis_index("rows")
    quad = lax.axis_index("quad")
    rows_here, lanes = sol.shape[1:]
    half = lanes // 2
    block = rows_here // span
    chunks = span // chunk_blocks
    chunk_rows = chunk_blocks * block
    odd = lax.rem(me, 2)
    partner = me + 1 - 2 * odd
    onward = lax.rem(me + 2 - 4 * odd + n, n)
    sends_on = jnp.where(odd == 1, me - 2 >= 0, me + 2 < n)
    gets_on = jnp.where(odd == 1, me + 2 < n, me - 2 >= 0)
    there = 2 * span * odd
    here = 2 * span - there

    def sol_copy(c):
        rows = pl.ds(c * chunk_rows, chunk_rows)
        return pltpu.make_async_copy(sol_hbm.at[:, rows], sol.at[:, rows], sol_sem.at[c])

    mass_copy = pltpu.make_async_copy(mass_hbm, mass, mass_sem)
    for c in range(chunks):
        sol_copy(c).start()
    mass_copy.start()

    barrier = pltpu.get_barrier_semaphore()
    pl.semaphore_signal(barrier, inc=1, device_id={"quad": 1 - quad}, device_id_type=MESH)
    if reduce_here:
        greeted = [lax.rem(me + o, n) for o in range(1, n)]
    else:
        greeted = [partner, lax.rem(me + 2, n), lax.rem(me + n - 2, n)]
    for device in greeted:
        pl.semaphore_signal(barrier, inc=1, device_id={"rows": device}, device_id_type=MESH)

    part = lax.broadcasted_iota(jnp.int32, (2 * 2 * owned * TILE, 2 * 2 * owned), 0)
    spread = jnp.where(
        part // TILE == lax.broadcasted_iota(jnp.int32, part.shape, 1), 1.0, 0.0
    ).astype(jnp.bfloat16)
    across = lax.broadcasted_iota(jnp.int32, (points * TILE, points), 0)
    spread_points = jnp.where(
        across // TILE == lax.broadcasted_iota(jnp.int32, across.shape, 1), 1.0, 0.0
    ).astype(jnp.bfloat16)
    tall = jnp.dot(spread, trig_ref[...], preferred_element_type=jnp.float32).astype(jnp.bfloat16)
    wide = lax.dot_general(
        tall, spread_points, (((1,), (1,)), ((), ())), preferred_element_type=jnp.float32
    )
    same = lax.rem(lax.broadcasted_iota(jnp.int32, wide.shape, 0), TILE) == lax.rem(
        lax.broadcasted_iota(jnp.int32, wide.shape, 1), TILE
    )
    weight[...] = jnp.where(same, wide, 0.0).astype(jnp.bfloat16)

    def quad_copy(c):
        rows = pl.ds(c * chunk_rows, chunk_rows)
        return pltpu.make_async_remote_copy(
            src_ref=theirs.at[:, rows], dst_ref=received.at[:, rows],
            send_sem=q_send.at[c], recv_sem=q_recv.at[c],
            device_id={"quad": 1 - quad}, device_id_type=MESH,
        )

    pieces = owned * chunks

    def at(q, base):
        return panels[q // chunks].at[pl.ds(base + q % chunks * chunk_blocks, chunk_blocks)]

    def cross(q, base):
        return pltpu.make_async_remote_copy(
            src_ref=at(q, span), dst_ref=at(q, base),
            send_sem=x_send.at[q], recv_sem=x_recv.at[q],
            device_id={"rows": partner}, device_id_type=MESH,
        )

    def forward(q, base):
        return pltpu.make_async_remote_copy(
            src_ref=at(q, here), dst_ref=at(q, base),
            send_sem=f_send.at[q], recv_sem=f_recv.at[q],
            device_id={"rows": onward}, device_id_type=MESH,
        )

    def relay(q):
        cross(q, there).wait_send()
        if q + WINDOW < pieces:
            cross(q + WINDOW, there).start()
        cross(q, here).wait_recv()

        @pl.when(sends_on)
        def _():
            forward(q, there).start()

    def arrived(k):
        @pl.when(gets_on)
        def _():
            for p in range(chunks):
                forward(k * chunks + p, there).wait_recv()

    def weigh(c):
        def body(g, carry):
            first = pl.multiple_of(c * chunk_rows + g * 2 * TILE, 2 * TILE)
            second = pl.multiple_of(first + TILE, TILE)
            stacked = jnp.concatenate(
                [
                    sol[:, pl.ds(first, TILE), :].reshape(points * TILE, lanes),
                    sol[:, pl.ds(second, TILE), :].reshape(points * TILE, lanes),
                ],
                axis=1,
            )
            z = jnp.dot(weight[...], stacked, preferred_element_type=jnp.float32)
            height = 2 * owned * TILE
            negative = lax.broadcasted_iota(jnp.int32, (height, lanes), 1) < half
            for h, start in ((0, first), (1, second)):
                straight = z[:height, h * lanes:(h + 1) * lanes]
                crossed = pltpu.roll(z[height:, h * lanes:(h + 1) * lanes], half, 1)
                value = straight + jnp.where(negative, -crossed, crossed)
                value = value.astype(jnp.bfloat16).reshape(2 * owned, TILE, lanes)
                own[:, pl.ds(start, TILE), :] = value[:owned]
                theirs[:, pl.ds(start, TILE), :] = value[owned:]
            return carry

        lax.fori_loop(0, chunk_rows // (2 * TILE), body, 0)

    def add_up(k, first, count):
        def body(b, carry):
            rows = pl.ds(pl.multiple_of(b * block, block), block)
            total = own[k, rows, :].astype(jnp.float32) + received[k, rows, :].astype(jnp.float32)
            panels[k][span + b] = total.astype(jnp.bfloat16)
            return carry

        lax.fori_loop(first, first + count, body, 0)

    def first_moment(c):
        quad_copy(c).wait_recv()
        add_up(0, c * chunk_blocks, chunk_blocks)
        if c < WINDOW:
            cross(c, there).start()

    for c in range(chunks):
        sol_copy(c).wait()
        weigh(c)
        if c == 0:
            pl.semaphore_wait(barrier, 1 + len(greeted))
        quad_copy(c).start()
        if c > 0:
            first_moment(c - 1)
    first_moment(chunks - 1)
    slots = mass.shape[1]
    offset = (me - 1) * span

    def apply_mass(k, first, last):
        panel = panels[k]

        def body(i, carry):
            left_side = jnp.concatenate([mass[i, j] for j in range(slots)], axis=1)
            right_side = jnp.concatenate(
                [panel[jnp.clip(cols_ref[i, j] - offset, 0, 3 * span - 1)] for j in range(slots)], axis=0
            )
            value = jnp.dot(left_side, right_side, preferred_element_type=jnp.float32)
            out_buf[k, pl.ds(pl.multiple_of(i * block, block), block), :] = value.astype(jnp.bfloat16)
            return carry

        lax.fori_loop(first, last, body, 0)

    def out_copy(k):
        return pltpu.make_async_copy(out_buf.at[k], out_hbm.at[k], out_sem.at[k])

    def rs_copy(k, o):
        return pltpu.make_async_remote_copy(
            src_ref=term.at[k, lax.rem(me + o, n)], dst_ref=rs_buf.at[k, o],
            send_sem=rs_send.at[k, o], recv_sem=rs_recv.at[k, o],
            device_id={"rows": lax.rem(me + o, n)}, device_id_type=MESH,
        )

    def ag_copy(k, o, origin):
        return pltpu.make_async_remote_copy(
            src_ref=red.at[k, origin], dst_ref=red.at[k, origin],
            send_sem=ag_send.at[k, o], recv_sem=ag_recv.at[k, o],
            device_id={"rows": lax.rem(me + o, n)}, device_id_type=MESH,
        )

    def project(k):
        value = jnp.dot(sources_ref[...], out_buf[k], preferred_element_type=jnp.float32)
        if reduce_here:
            term[k] = value.reshape(term.shape[1:])
            for o in range(1, n):
                rs_copy(k, o).start()
        else:
            red_out[k] = value

    def reduce(k):
        total = term[k, me]
        for o in range(1, n):
            rs_copy(k, o).wait_recv()
            total = total + rs_buf[k, o]
        red[k, me] = total
        for o in range(1, n):
            ag_copy(k, o, me).start()

    def finish(k):
        out_copy(k).start()
        project(k)

    cuts = [0, 4, 7, span]
    for k in range(owned):
        for p in range(chunks):
            q = k * chunks + p
            if k == 0 and p < owned - 1:
                add_up(p + 1, 0, span)
            relay(q)
            if k > 0 and p >= 2:
                if p == 2:
                    arrived(k - 1)
                    if k == 1:
                        mass_copy.wait()
                apply_mass(k - 1, cuts[p - 2], cuts[p - 1])
        if k > 0:
            finish(k - 1)
        if reduce_here and k > 1:
            reduce(k - 2)
    arrived(owned - 1)
    apply_mass(owned - 1, 0, span)
    finish(owned - 1)
    if reduce_here:
        reduce(owned - 2)
        reduce(owned - 1)

    @pl.when(sends_on)
    def _():
        for q in range(pieces):
            forward(q, there).wait_send()

    for c in range(chunks):
        quad_copy(c).wait_send()
    for k in range(owned):
        out_copy(k).wait()
        if reduce_here:
            for o in range(1, n):
                rs_copy(k, o).wait_send()
                ag_copy(k, o, me).wait_send()
                ag_copy(k, o, lax.rem(me + n - o, n)).wait_recv()
            red_out[k] = red[k].reshape(red_out.shape[1:])


def local(n, quads, solutions, point_of_slot, mass_blocks, block_cols, sources):
    points, rows_here, lanes = solutions.shape
    width = lanes // 2
    span, slots, block_size = mass_blocks.shape[:3]
    owned = MOMENTS // quads
    total_points = points * quads
    chunk_blocks = 2
    chunks = span // chunk_blocks
    reduce_here = n <= 8 and width % n == 0
    parts = n if reduce_here else 1
    theta = 2.0 * math.pi * (point_of_slot.astype(jnp.float32) + 0.5) / total_points
    order = (jnp.arange(MOMENTS) + owned * lax.axis_index("quad")) % MOMENTS
    angles = (order + 1).astype(jnp.float32)[:, None] * theta[None, :]
    cosine = (jnp.cos(angles) / total_points).astype(jnp.bfloat16)
    sine = (jnp.sin(angles) / total_points).astype(jnp.bfloat16)
    both = jnp.concatenate([cosine, sine], axis=0)
    bf16, f32 = jnp.bfloat16, jnp.float32
    dma = pltpu.SemaphoreType.DMA
    pieces = chunks * owned
    vmem = pl.BlockSpec(memory_space=pltpu.VMEM)
    hbm = pl.BlockSpec(memory_space=pl.ANY)
    mass_applied, reduced = pl.pallas_call(
        functools.partial(kernel, n, quads, span, owned, points, chunk_blocks, reduce_here),
        out_shape=(
            jax.ShapeDtypeStruct((owned, rows_here, lanes), bf16),
            jax.ShapeDtypeStruct((owned, width, lanes), f32),
        ),
        in_specs=[vmem, pl.BlockSpec(memory_space=pltpu.SMEM), vmem, hbm, hbm],
        out_specs=(hbm, vmem),
        scratch_shapes=[
            pltpu.VMEM(solutions.shape, bf16),
            pltpu.VMEM(mass_blocks.shape, bf16),
            pltpu.VMEM((2 * MOMENTS * TILE, points * TILE), bf16),
            pltpu.VMEM((owned, rows_here, lanes), bf16),
            pltpu.VMEM((owned, rows_here, lanes), bf16),
            pltpu.VMEM((owned, rows_here, lanes), bf16),
            pltpu.VMEM((owned, rows_here, lanes), bf16),
            pltpu.VMEM((owned, parts, width // parts, lanes), f32),
            pltpu.VMEM((owned, parts, width // parts, lanes), f32),
            pltpu.VMEM((owned, parts, width // parts, lanes), f32),
        ]
        + [pltpu.VMEM((3 * span, block_size, lanes), bf16) for _ in range(owned)]
        + [
            dma((chunks,)), dma, dma((owned,)), dma((chunks,)), dma((chunks,)),
            dma((pieces,)), dma((pieces,)), dma((pieces,)), dma((pieces,)),
            dma((owned, parts)), dma((owned, parts)), dma((owned, parts)), dma((owned, parts)),
        ],
        compiler_params=pltpu.CompilerParams(
            collective_id=0, has_side_effects=True, vmem_limit_bytes=48 * 1024 * 1024
        ),
    )(both, block_cols, sources.T, solutions, mass_blocks)
    if not reduce_here:
        reduced = lax.psum(reduced, "rows")
    return mass_applied, reduced


def solution(mesh):
    in_specs = (
        P("quad", ("group", "rows"), None),
        P(("group", "quad")),
        P(("group", "rows"), None, None, None),
        P(("group", "rows"), None),
        P(("group", "rows"), None),
    )
    out_specs = (P("quad", ("group", "rows"), None), P(("group", "quad"), None, None))
    step = functools.partial(local, mesh.shape["rows"], mesh.shape["quad"])
    return jax.shard_map(step, mesh=mesh, in_specs=in_specs, out_specs=out_specs, check_vma=False)
```

```python
import functools
import math

import jax
import jax.numpy as jnp
from jax import lax
from jax.experimental import pallas as pl
from jax.experimental.pallas import tpu as pltpu
from jax.sharding import PartitionSpec as P

MOMENTS = 8
TILE = 16
WINDOW = 3
MESH = pl.DeviceIdType.MESH


def kernel(
    n, quads, span, owned, points, chunk_blocks, reduce_here,
    trig_ref, cols_ref, sources_ref, sol_hbm, mass_hbm,
    out_hbm, red_out,
    sol, mass, weight, own, theirs, received, out_buf, term, rs_buf, red, *rest,
):
    panels = rest[:owned]
    (sol_sem, mass_sem, out_sem, q_send, q_recv, x_send, x_recv, f_send, f_recv,
     rs_send, rs_recv, ag_send, ag_recv) = rest[owned:]
    me = lax.axis_index("rows")
    quad = lax.axis_index("quad")
    rows_here, lanes = sol.shape[1:]
    half = lanes // 2
    block = rows_here // span
    chunks = span // chunk_blocks
    chunk_rows = chunk_blocks * block
    odd = lax.rem(me, 2)
    partner = me + 1 - 2 * odd
    onward = lax.rem(me + 2 - 4 * odd + n, n)
    sends_on = jnp.where(odd == 1, me - 2 >= 0, me + 2 < n)
    gets_on = jnp.where(odd == 1, me + 2 < n, me - 2 >= 0)
    there = 2 * span * odd
    here = 2 * span - there

    def sol_copy(c):
        rows = pl.ds(c * chunk_rows, chunk_rows)
        return pltpu.make_async_copy(sol_hbm.at[:, rows], sol.at[:, rows], sol_sem.at[c])

    mass_copy = pltpu.make_async_copy(mass_hbm, mass, mass_sem)
    for c in range(chunks):
        sol_copy(c).start()
    mass_copy.start()

    barrier = pltpu.get_barrier_semaphore()
    pl.semaphore_signal(barrier, inc=1, device_id={"quad": 1 - quad}, device_id_type=MESH)
    if reduce_here:
        greeted = [lax.rem(me + o, n) for o in range(1, n)]
    else:
        greeted = [partner, lax.rem(me + 2, n), lax.rem(me + n - 2, n)]
    for device in greeted:
        pl.semaphore_signal(barrier, inc=1, device_id={"rows": device}, device_id_type=MESH)

    part = lax.broadcasted_iota(jnp.int32, (2 * 2 * owned * TILE, 2 * 2 * owned), 0)
    spread = jnp.where(
        part // TILE == lax.broadcasted_iota(jnp.int32, part.shape, 1), 1.0, 0.0
    ).astype(jnp.bfloat16)
    across = lax.broadcasted_iota(jnp.int32, (points * TILE, points), 0)
    spread_points = jnp.where(
        across // TILE == lax.broadcasted_iota(jnp.int32, across.shape, 1), 1.0, 0.0
    ).astype(jnp.bfloat16)
    tall = jnp.dot(spread, trig_ref[...], preferred_element_type=jnp.float32).astype(jnp.bfloat16)
    wide = lax.dot_general(
        tall, spread_points, (((1,), (1,)), ((), ())), preferred_element_type=jnp.float32
    )
    same = lax.rem(lax.broadcasted_iota(jnp.int32, wide.shape, 0), TILE) == lax.rem(
        lax.broadcasted_iota(jnp.int32, wide.shape, 1), TILE
    )
    weight[...] = jnp.where(same, wide, 0.0).astype(jnp.bfloat16)

    def quad_copy(c):
        rows = pl.ds(c * chunk_rows, chunk_rows)
        return pltpu.make_async_remote_copy(
            src_ref=theirs.at[:, rows], dst_ref=received.at[:, rows],
            send_sem=q_send.at[c], recv_sem=q_recv.at[c],
            device_id={"quad": 1 - quad}, device_id_type=MESH,
        )

    pieces = owned * chunks
    early = 2
    order = [(k, c) for c in range(chunks) for k in range(early)]
    order += [(k, c) for k in range(early, owned) for c in range(chunks)]

    def at(q, base):
        k, c = order[q]
        return panels[k].at[pl.ds(base + c * chunk_blocks, chunk_blocks)]

    def cross(q, base):
        return pltpu.make_async_remote_copy(
            src_ref=at(q, span), dst_ref=at(q, base),
            send_sem=x_send.at[q], recv_sem=x_recv.at[q],
            device_id={"rows": partner}, device_id_type=MESH,
        )

    def forward(q, base):
        return pltpu.make_async_remote_copy(
            src_ref=at(q, here), dst_ref=at(q, base),
            send_sem=f_send.at[q], recv_sem=f_recv.at[q],
            device_id={"rows": onward}, device_id_type=MESH,
        )

    def relay(q):
        cross(q, there).wait_send()
        if early * chunks <= q + WINDOW < pieces:
            cross(q + WINDOW, there).start()
        cross(q, here).wait_recv()

        @pl.when(sends_on)
        def _():
            forward(q, there).start()

    def arrived(k):
        @pl.when(gets_on)
        def _():
            for p in range(chunks):
                forward(order.index((k, p)), there).wait_recv()

    def weigh(c):
        def pair(g):
            first = pl.multiple_of(c * chunk_rows + g * 2 * TILE, 2 * TILE)
            second = pl.multiple_of(first + TILE, TILE)
            stacked = jnp.concatenate(
                [
                    sol[:, pl.ds(first, TILE), :].reshape(points * TILE, lanes),
                    sol[:, pl.ds(second, TILE), :].reshape(points * TILE, lanes),
                ],
                axis=1,
            )
            z = jnp.dot(weight[...], stacked, preferred_element_type=jnp.float32)
            height = 2 * owned * TILE
            negative = lax.broadcasted_iota(jnp.int32, (height, lanes), 1) < half
            for h, start in ((0, first), (1, second)):
                straight = z[:height, h * lanes:(h + 1) * lanes]
                crossed = pltpu.roll(z[height:, h * lanes:(h + 1) * lanes], half, 1)
                value = straight + jnp.where(negative, -crossed, crossed)
                value = value.astype(jnp.bfloat16).reshape(2 * owned, TILE, lanes)
                own[:, pl.ds(start, TILE), :] = value[:owned]
                theirs[:, pl.ds(start, TILE), :] = value[owned:]

        def body(g, carry):
            pair(2 * g)
            pair(2 * g + 1)
            return carry

        lax.fori_loop(0, chunk_rows // (4 * TILE), body, 0)

    def add_up(k, first, count):
        def body(b, carry):
            rows = pl.ds(pl.multiple_of(b * block, block), block)
            total = own[k, rows, :].astype(jnp.float32) + received[k, rows, :].astype(jnp.float32)
            panels[k][span + b] = total.astype(jnp.bfloat16)
            return carry

        lax.fori_loop(first, first + count, body, 0)

    def first_moment(c):
        quad_copy(c).wait_recv()
        for k in range(early):
            add_up(k, c * chunk_blocks, chunk_blocks)
            cross(order.index((k, c)), there).start()

    for c in range(chunks):
        sol_copy(c).wait()
        weigh(c)
        if c == 0:
            pl.semaphore_wait(barrier, 1 + len(greeted))
        quad_copy(c).start()
        if c > 0:
            first_moment(c - 1)
    first_moment(chunks - 1)
    slots = mass.shape[1]
    offset = (me - 1) * span

    def apply_mass(k, first, last):
        panel = panels[k]

        def block_row(i):
            left_side = jnp.concatenate([mass[i, j] for j in range(slots)], axis=1)
            right_side = jnp.concatenate(
                [panel[jnp.clip(cols_ref[i, j] - offset, 0, 3 * span - 1)] for j in range(slots)],
                axis=0,
            )
            value = jnp.dot(left_side, right_side, preferred_element_type=jnp.float32)
            out_buf[k, pl.ds(pl.multiple_of(i * block, block), block), :] = value.astype(jnp.bfloat16)

        def body(i, carry):
            block_row(2 * i)
            block_row(2 * i + 1)
            return carry

        lax.fori_loop(first // 2, last // 2, body, 0)

    def out_copy(k):
        return pltpu.make_async_copy(out_buf.at[k], out_hbm.at[k], out_sem.at[k])

    batches = [pl.ds(0, owned - 1), pl.ds(owned - 1, 1)]

    def rs_copy(b, o):
        return pltpu.make_async_remote_copy(
            src_ref=term.at[batches[b], lax.rem(me + o, n)], dst_ref=rs_buf.at[batches[b], o],
            send_sem=rs_send.at[b, o], recv_sem=rs_recv.at[b, o],
            device_id={"rows": lax.rem(me + o, n)}, device_id_type=MESH,
        )

    def ag_copy(b, o, origin):
        return pltpu.make_async_remote_copy(
            src_ref=red.at[batches[b], origin], dst_ref=red.at[batches[b], origin],
            send_sem=ag_send.at[b, o], recv_sem=ag_recv.at[b, o],
            device_id={"rows": lax.rem(me + o, n)}, device_id_type=MESH,
        )

    def finish(k):
        out_copy(k).start()
        value = jnp.dot(sources_ref[...], out_buf[k], preferred_element_type=jnp.float32)
        if not reduce_here:
            red_out[k] = value
            return
        term[k] = value.reshape(term.shape[1:])
        if k >= owned - 2:
            for o in range(1, n):
                rs_copy(k - (owned - 2), o).start()

    def reduce(b):
        total = term[batches[b], me]
        for o in range(1, n):
            rs_copy(b, o).wait_recv()
            total = total + rs_buf[batches[b], o]
        red[batches[b], me] = total
        for o in range(1, n):
            ag_copy(b, o, me).start()

    cuts = [0, 4, 8, span]
    steps = len(cuts) - 1
    for q in range(pieces):
        relay(q)
        if q % 2 == 1 and early + q // 2 < owned:
            add_up(early + q // 2, 0, span)
        if q == early * chunks:
            mass_copy.wait()
        k, step = divmod(q - early * chunks, steps)
        if 0 <= k < owned - 1:
            if step == 0:
                arrived(k)
            apply_mass(k, cuts[step], cuts[step + 1])
            if step == steps - 1:
                finish(k)
    arrived(owned - 1)
    apply_mass(owned - 1, 0, span)
    finish(owned - 1)
    if reduce_here:
        reduce(0)
        reduce(1)

    @pl.when(sends_on)
    def _():
        for q in range(pieces):
            forward(q, there).wait_send()

    for c in range(chunks):
        quad_copy(c).wait_send()
    for k in range(owned):
        out_copy(k).wait()
    if reduce_here:
        for b in range(len(batches)):
            for o in range(1, n):
                rs_copy(b, o).wait_send()
                ag_copy(b, o, me).wait_send()
                ag_copy(b, o, lax.rem(me + n - o, n)).wait_recv()
        for k in range(owned):
            red_out[k] = red[k].reshape(red_out.shape[1:])


def local(n, quads, solutions, point_of_slot, mass_blocks, block_cols, sources):
    points, rows_here, lanes = solutions.shape
    width = lanes // 2
    span, slots, block_size = mass_blocks.shape[:3]
    owned = MOMENTS // quads
    total_points = points * quads
    chunk_blocks = 2
    chunks = span // chunk_blocks
    reduce_here = n <= 8 and width % n == 0
    parts = n if reduce_here else 1
    theta = 2.0 * math.pi * (point_of_slot.astype(jnp.float32) + 0.5) / total_points
    order = (jnp.arange(MOMENTS) + owned * lax.axis_index("quad")) % MOMENTS
    angles = (order + 1).astype(jnp.float32)[:, None] * theta[None, :]
    cosine = (jnp.cos(angles) / total_points).astype(jnp.bfloat16)
    sine = (jnp.sin(angles) / total_points).astype(jnp.bfloat16)
    both = jnp.concatenate([cosine, sine], axis=0)
    bf16, f32 = jnp.bfloat16, jnp.float32
    dma = pltpu.SemaphoreType.DMA
    pieces = chunks * owned
    vmem = pl.BlockSpec(memory_space=pltpu.VMEM)
    hbm = pl.BlockSpec(memory_space=pl.ANY)
    mass_applied, reduced = pl.pallas_call(
        functools.partial(kernel, n, quads, span, owned, points, chunk_blocks, reduce_here),
        out_shape=(
            jax.ShapeDtypeStruct((owned, rows_here, lanes), bf16),
            jax.ShapeDtypeStruct((owned, width, lanes), f32),
        ),
        in_specs=[vmem, pl.BlockSpec(memory_space=pltpu.SMEM), vmem, hbm, hbm],
        out_specs=(hbm, vmem),
        scratch_shapes=[
            pltpu.VMEM(solutions.shape, bf16),
            pltpu.VMEM(mass_blocks.shape, bf16),
            pltpu.VMEM((2 * MOMENTS * TILE, points * TILE), bf16),
            pltpu.VMEM((owned, rows_here, lanes), bf16),
            pltpu.VMEM((owned, rows_here, lanes), bf16),
            pltpu.VMEM((owned, rows_here, lanes), bf16),
            pltpu.VMEM((owned, rows_here, lanes), bf16),
            pltpu.VMEM((owned, parts, width // parts, lanes), f32),
            pltpu.VMEM((owned, parts, width // parts, lanes), f32),
            pltpu.VMEM((owned, parts, width // parts, lanes), f32),
        ]
        + [pltpu.VMEM((3 * span, block_size, lanes), bf16) for _ in range(owned)]
        + [
            dma((chunks,)), dma, dma((owned,)), dma((chunks,)), dma((chunks,)),
            dma((pieces,)), dma((pieces,)), dma((pieces,)), dma((pieces,)),
            dma((owned, parts)), dma((owned, parts)), dma((owned, parts)), dma((owned, parts)),
        ],
        compiler_params=pltpu.CompilerParams(
            collective_id=0, has_side_effects=True, vmem_limit_bytes=48 * 1024 * 1024
        ),
    )(both, block_cols, sources.T, solutions, mass_blocks)
    if not reduce_here:
        reduced = lax.psum(reduced, "rows")
    return mass_applied, reduced


def solution(mesh):
    in_specs = (
        P("quad", ("group", "rows"), None),
        P(("group", "quad")),
        P(("group", "rows"), None, None, None),
        P(("group", "rows"), None),
        P(("group", "rows"), None),
    )
    out_specs = (P("quad", ("group", "rows"), None), P(("group", "quad"), None, None))
    step = functools.partial(local, mesh.shape["rows"], mesh.shape["quad"])
    return jax.shard_map(step, mesh=mesh, in_specs=in_specs, out_specs=out_specs, check_vma=False)
```

```python
import functools
import math

import jax
import jax.numpy as jnp
from jax import lax
from jax.experimental import pallas as pl
from jax.experimental.pallas import tpu as pltpu
from jax.sharding import PartitionSpec as P

MOMENTS = 8
TILE = 16
WINDOW = 5
MESH = pl.DeviceIdType.MESH


def kernel(
    n, quads, span, owned, points, chunk_blocks, reduce_here,
    trig_ref, cols_ref, sources_ref, sol_hbm, mass_hbm,
    out_hbm, red_out,
    sol, mass, weight, own, theirs, received, out_buf, term, rs_buf, red, *rest,
):
    panels = rest[:owned]
    (sol_sem, mass_sem, out_sem, q_send, q_recv, x_send, x_recv, f_send, f_recv,
     rs_send, rs_recv, ag_send, ag_recv) = rest[owned:]
    me = lax.axis_index("rows")
    quad = lax.axis_index("quad")
    rows_here, lanes = sol.shape[1:]
    half = lanes // 2
    block = rows_here // span
    chunks = span // chunk_blocks
    chunk_rows = chunk_blocks * block
    odd = lax.rem(me, 2)
    partner = me + 1 - 2 * odd
    onward = lax.rem(me + 2 - 4 * odd + n, n)
    sends_on = jnp.where(odd == 1, me - 2 >= 0, me + 2 < n)
    gets_on = jnp.where(odd == 1, me + 2 < n, me - 2 >= 0)
    there = 2 * span * odd
    here = 2 * span - there

    def sol_copy(c):
        rows = pl.ds(c * chunk_rows, chunk_rows)
        return pltpu.make_async_copy(sol_hbm.at[:, rows], sol.at[:, rows], sol_sem.at[c])

    mass_copy = pltpu.make_async_copy(mass_hbm, mass, mass_sem)
    for c in range(chunks):
        sol_copy(c).start()
    mass_copy.start()

    barrier = pltpu.get_barrier_semaphore()
    pl.semaphore_signal(barrier, inc=1, device_id={"quad": 1 - quad}, device_id_type=MESH)
    if reduce_here:
        greeted = [lax.rem(me + o, n) for o in range(1, n)]
    else:
        greeted = [partner, lax.rem(me + 2, n), lax.rem(me + n - 2, n)]
    for device in greeted:
        pl.semaphore_signal(barrier, inc=1, device_id={"rows": device}, device_id_type=MESH)

    part = lax.broadcasted_iota(jnp.int32, (2 * 2 * owned * TILE, 2 * 2 * owned), 0)
    spread = jnp.where(
        part // TILE == lax.broadcasted_iota(jnp.int32, part.shape, 1), 1.0, 0.0
    ).astype(jnp.bfloat16)
    across = lax.broadcasted_iota(jnp.int32, (points * TILE, points), 0)
    spread_points = jnp.where(
        across // TILE == lax.broadcasted_iota(jnp.int32, across.shape, 1), 1.0, 0.0
    ).astype(jnp.bfloat16)
    tall = jnp.dot(spread, trig_ref[...], preferred_element_type=jnp.float32).astype(jnp.bfloat16)
    wide = lax.dot_general(
        tall, spread_points, (((1,), (1,)), ((), ())), preferred_element_type=jnp.float32
    )
    same = lax.rem(lax.broadcasted_iota(jnp.int32, wide.shape, 0), TILE) == lax.rem(
        lax.broadcasted_iota(jnp.int32, wide.shape, 1), TILE
    )
    weight[...] = jnp.where(same, wide, 0.0).astype(jnp.bfloat16)

    def quad_copy(c):
        rows = pl.ds(c * chunk_rows, chunk_rows)
        return pltpu.make_async_remote_copy(
            src_ref=theirs.at[:, rows], dst_ref=received.at[:, rows],
            send_sem=q_send.at[c], recv_sem=q_recv.at[c],
            device_id={"quad": 1 - quad}, device_id_type=MESH,
        )

    pieces = owned * chunks
    early = 2
    order = [(k, c) for c in range(chunks) for k in range(early)]
    order += [(k, c) for k in range(early, owned) for c in range(chunks)]

    def at(q, base):
        k, c = order[q]
        return panels[k].at[pl.ds(base + c * chunk_blocks, chunk_blocks)]

    def cross(q, base):
        return pltpu.make_async_remote_copy(
            src_ref=at(q, span), dst_ref=at(q, base),
            send_sem=x_send.at[q], recv_sem=x_recv.at[q],
            device_id={"rows": partner}, device_id_type=MESH,
        )

    def forward(q, base):
        return pltpu.make_async_remote_copy(
            src_ref=at(q, here), dst_ref=at(q, base),
            send_sem=f_send.at[q], recv_sem=f_recv.at[q],
            device_id={"rows": onward}, device_id_type=MESH,
        )

    def relay(q):
        cross(q, there).wait_send()
        if early * chunks <= q + WINDOW < pieces:
            cross(q + WINDOW, there).start()
        cross(q, here).wait_recv()

        @pl.when(sends_on)
        def _():
            forward(q, there).start()

    def arrived(k):
        @pl.when(gets_on)
        def _():
            for p in range(chunks):
                forward(order.index((k, p)), there).wait_recv()

    def weigh(c):
        def pair(g):
            first = pl.multiple_of(c * chunk_rows + g * 2 * TILE, 2 * TILE)
            second = pl.multiple_of(first + TILE, TILE)
            stacked = jnp.concatenate(
                [
                    sol[:, pl.ds(first, TILE), :].reshape(points * TILE, lanes),
                    sol[:, pl.ds(second, TILE), :].reshape(points * TILE, lanes),
                ],
                axis=1,
            )
            z = jnp.dot(weight[...], stacked, preferred_element_type=jnp.float32)
            height = 2 * owned * TILE
            negative = lax.broadcasted_iota(jnp.int32, (height, lanes), 1) < half
            for h, start in ((0, first), (1, second)):
                straight = z[:height, h * lanes:(h + 1) * lanes]
                crossed = pltpu.roll(z[height:, h * lanes:(h + 1) * lanes], half, 1)
                value = straight + jnp.where(negative, -crossed, crossed)
                value = value.astype(jnp.bfloat16).reshape(2 * owned, TILE, lanes)
                own[:, pl.ds(start, TILE), :] = value[:owned]
                theirs[:, pl.ds(start, TILE), :] = value[owned:]

        def body(g, carry):
            pair(2 * g)
            pair(2 * g + 1)
            return carry

        lax.fori_loop(0, chunk_rows // (4 * TILE), body, 0)

    def add_up(k, first, count):
        def body(b, carry):
            rows = pl.ds(pl.multiple_of(b * block, block), block)
            total = own[k, rows, :].astype(jnp.float32) + received[k, rows, :].astype(jnp.float32)
            panels[k][span + b] = total.astype(jnp.bfloat16)
            return carry

        lax.fori_loop(first, first + count, body, 0)

    def first_moment(c):
        quad_copy(c).wait_recv()
        for k in range(early):
            add_up(k, c * chunk_blocks, chunk_blocks)
            cross(order.index((k, c)), there).start()

    for c in range(chunks):
        sol_copy(c).wait()
        weigh(c)
        if c == 0:
            pl.semaphore_wait(barrier, 1 + len(greeted))
        quad_copy(c).start()
        if c > 0:
            first_moment(c - 1)
    first_moment(chunks - 1)
    slots = mass.shape[1]
    offset = (me - 1) * span

    def apply_mass(k, first, last):
        panel = panels[k]

        def block_row(i):
            left_side = jnp.concatenate([mass[i, j] for j in range(slots)], axis=1)
            right_side = jnp.concatenate(
                [panel[jnp.clip(cols_ref[i, j] - offset, 0, 3 * span - 1)] for j in range(slots)],
                axis=0,
            )
            value = jnp.dot(left_side, right_side, preferred_element_type=jnp.float32)
            out_buf[k, pl.ds(pl.multiple_of(i * block, block), block), :] = value.astype(jnp.bfloat16)

        def body(i, carry):
            block_row(2 * i)
            block_row(2 * i + 1)
            return carry

        lax.fori_loop(first // 2, last // 2, body, 0)

    def out_copy(k):
        return pltpu.make_async_copy(out_buf.at[k], out_hbm.at[k], out_sem.at[k])

    batches = [pl.ds(0, owned - 1), pl.ds(owned - 1, 1)]

    def rs_copy(b, o):
        return pltpu.make_async_remote_copy(
            src_ref=term.at[batches[b], lax.rem(me + o, n)], dst_ref=rs_buf.at[batches[b], o],
            send_sem=rs_send.at[b, o], recv_sem=rs_recv.at[b, o],
            device_id={"rows": lax.rem(me + o, n)}, device_id_type=MESH,
        )

    def ag_copy(b, o, origin):
        return pltpu.make_async_remote_copy(
            src_ref=red.at[batches[b], origin], dst_ref=red.at[batches[b], origin],
            send_sem=ag_send.at[b, o], recv_sem=ag_recv.at[b, o],
            device_id={"rows": lax.rem(me + o, n)}, device_id_type=MESH,
        )

    def finish(k):
        out_copy(k).start()
        value = jnp.dot(sources_ref[...], out_buf[k], preferred_element_type=jnp.float32)
        if not reduce_here:
            red_out[k] = value
            return
        term[k] = value.reshape(term.shape[1:])
        if k >= owned - 2:
            for o in range(1, n):
                rs_copy(k - (owned - 2), o).start()

    def reduce(b):
        total = term[batches[b], me]
        for o in range(1, n):
            rs_copy(b, o).wait_recv()
            total = total + rs_buf[batches[b], o]
        red[batches[b], me] = total
        for o in range(1, n):
            ag_copy(b, o, me).start()

    cuts = [0, 4, 8, span]
    steps = len(cuts) - 1
    for q in range(pieces):
        relay(q)
        if q % 2 == 1 and early + q // 2 < owned:
            add_up(early + q // 2, 0, span)
        if q == early * chunks:
            mass_copy.wait()
        k, step = divmod(q - early * chunks, steps)
        if 0 <= k < owned - 1:
            if step == 0:
                arrived(k)
            apply_mass(k, cuts[step], cuts[step + 1])
            if step == steps - 1:
                finish(k)
    arrived(owned - 1)
    apply_mass(owned - 1, 0, cuts[2])
    if reduce_here:
        reduce(0)
    apply_mass(owned - 1, cuts[2], span)
    finish(owned - 1)
    if reduce_here:
        reduce(1)

    @pl.when(sends_on)
    def _():
        for q in range(pieces):
            forward(q, there).wait_send()

    for c in range(chunks):
        quad_copy(c).wait_send()
    for k in range(owned):
        out_copy(k).wait()
    if reduce_here:
        for b in range(len(batches)):
            for o in range(1, n):
                rs_copy(b, o).wait_send()
                ag_copy(b, o, me).wait_send()
                ag_copy(b, o, lax.rem(me + n - o, n)).wait_recv()
        for k in range(owned):
            red_out[k] = red[k].reshape(red_out.shape[1:])


def local(n, quads, solutions, point_of_slot, mass_blocks, block_cols, sources):
    points, rows_here, lanes = solutions.shape
    width = lanes // 2
    span, slots, block_size = mass_blocks.shape[:3]
    owned = MOMENTS // quads
    total_points = points * quads
    chunk_blocks = 2
    chunks = span // chunk_blocks
    reduce_here = n <= 8 and width % n == 0
    parts = n if reduce_here else 1
    theta = 2.0 * math.pi * (point_of_slot.astype(jnp.float32) + 0.5) / total_points
    order = (jnp.arange(MOMENTS) + owned * lax.axis_index("quad")) % MOMENTS
    angles = (order + 1).astype(jnp.float32)[:, None] * theta[None, :]
    cosine = (jnp.cos(angles) / total_points).astype(jnp.bfloat16)
    sine = (jnp.sin(angles) / total_points).astype(jnp.bfloat16)
    both = jnp.concatenate([cosine, sine], axis=0)
    bf16, f32 = jnp.bfloat16, jnp.float32
    dma = pltpu.SemaphoreType.DMA
    pieces = chunks * owned
    vmem = pl.BlockSpec(memory_space=pltpu.VMEM)
    hbm = pl.BlockSpec(memory_space=pl.ANY)
    mass_applied, reduced = pl.pallas_call(
        functools.partial(kernel, n, quads, span, owned, points, chunk_blocks, reduce_here),
        out_shape=(
            jax.ShapeDtypeStruct((owned, rows_here, lanes), bf16),
            jax.ShapeDtypeStruct((owned, width, lanes), f32),
        ),
        in_specs=[vmem, pl.BlockSpec(memory_space=pltpu.SMEM), vmem, hbm, hbm],
        out_specs=(hbm, vmem),
        scratch_shapes=[
            pltpu.VMEM(solutions.shape, bf16),
            pltpu.VMEM(mass_blocks.shape, bf16),
            pltpu.VMEM((2 * MOMENTS * TILE, points * TILE), bf16),
            pltpu.VMEM((owned, rows_here, lanes), bf16),
            pltpu.VMEM((owned, rows_here, lanes), bf16),
            pltpu.VMEM((owned, rows_here, lanes), bf16),
            pltpu.VMEM((owned, rows_here, lanes), bf16),
            pltpu.VMEM((owned, parts, width // parts, lanes), f32),
            pltpu.VMEM((owned, parts, width // parts, lanes), f32),
            pltpu.VMEM((owned, parts, width // parts, lanes), f32),
        ]
        + [pltpu.VMEM((3 * span, block_size, lanes), bf16) for _ in range(owned)]
        + [
            dma((chunks,)), dma, dma((owned,)), dma((chunks,)), dma((chunks,)),
            dma((pieces,)), dma((pieces,)), dma((pieces,)), dma((pieces,)),
            dma((owned, parts)), dma((owned, parts)), dma((owned, parts)), dma((owned, parts)),
        ],
        compiler_params=pltpu.CompilerParams(
            collective_id=0, has_side_effects=True, vmem_limit_bytes=48 * 1024 * 1024
        ),
    )(both, block_cols, sources.T, solutions, mass_blocks)
    if not reduce_here:
        reduced = lax.psum(reduced, "rows")
    return mass_applied, reduced


def solution(mesh):
    in_specs = (
        P("quad", ("group", "rows"), None),
        P(("group", "quad")),
        P(("group", "rows"), None, None, None),
        P(("group", "rows"), None),
        P(("group", "rows"), None),
    )
    out_specs = (P("quad", ("group", "rows"), None), P(("group", "quad"), None, None))
    step = functools.partial(local, mesh.shape["rows"], mesh.shape["quad"])
    return jax.shard_map(step, mesh=mesh, in_specs=in_specs, out_specs=out_specs, check_vma=False)
```
